32 devices in a mesh: groups: 1, frames: 32 (over z, y, x, core).
Axes of the slice: x: 2, y: 2, z: 4, core: 2. Of those that a mesh axis runs over, the one named last changes fastest.
Arguments:
- features: bfloat16 [32, 4096, 256], P(('groups', 'frames')), may hold values from -6 to 6
- query_frame: int32 [128], P('groups'), may hold values from 0 to 31
- query_pos: int32 [128], P('groups'), may hold values from 0 to 4095
- frame_order: int32 [32], P('groups'), may hold values from 0 to 31, each once
- conv1_weight: float32 [16, 9], replicated, may hold values from -2 to 2
- conv1_bias: float32 [16], replicated, may hold values from -0.5 to 0.5
- conv2_weight: bfloat16 [32, 16, 2, 2], replicated, may hold values from -0.75 to 0.75
- proj_weight: bfloat16 [2048, 512], replicated, may hold values from -0.125 to 0.125
- norm_gains: float32 [2, 2, 512], replicated, may hold values from 0.25 to 1.75
- time_kernels: float32 [2, 3, 512], replicated, may hold values from -3 to 3
- mix_up: bfloat16 [2, 512, 2048], replicated, may hold values from -0.25 to 0.25
- mix_down: bfloat16 [2, 2048, 512], replicated, may hold values from -0.125 to 0.125
Outputs:
- mixed: bfloat16 [32, 128, 512], P(('groups', 'frames'))
The draws below stay inside these ranges and needn't reach their ends.
Inputs may be any that keep to these rules, and one draw needn't show every extreme that they name: query_pos = y * 64 + x. `frame_order`: a permutation: every time index once.
All inputs are finite; a program needn't handle non-finite values.
Results may differ from the reference program's by a relative error of at most 0.015.
Values may be sent and summed in bfloat16 or wider, within the bound.
A program may use at most 128 MiB of HBM per device.

```python
import jax
import jax.numpy as jnp
from jax import lax

MAP = 64
C = 256
CH1 = 16
CH2 = 32
GRID = 8
P_SIZE = 512
HID = 2048
BLOCKS = 2
FRAMES = 32
TRACKS = 128


def place_ends(result, own_key, least, top_value):
    shape = result.shape
    place = [jax.random.randint(jax.random.fold_in(own_key, axis), (), 0, shape[axis]) for axis in range(len(shape))]
    result = result.at[tuple(place)].set(least)
    longest = shape.index(max(shape))
    place[longest] = (place[longest] + 1) % shape[longest]
    return result.at[tuple(place)].set(top_value)


def block_scale(key, extent, cuts, low, high):
    def one(dim, shards_of):
        draws = jax.random.uniform(jax.random.fold_in(jax.random.fold_in(key, 6), dim), (shards_of,), jnp.float32, low / len(cuts), high / len(cuts))
        return jnp.repeat(jnp.exp(draws), extent[dim] // shards_of).reshape((-1,) + (1,) * (len(extent) - dim - 1))

    loudness = one(*cuts[0])
    for cut in cuts[1:]:
        loudness = loudness * one(*cut)
    return loudness


def normal_values(rng, dims, deviation, limit, pieces=(), kind=jnp.bfloat16):
    result = jax.random.normal(rng, dims, jnp.float32) * deviation
    if len(pieces) > 0:
        result = block_scale(rng, dims, pieces, -0.22, 0.18) * result
    return jnp.clip(result, min=-limit, max=limit).astype(kind)


def setup_inputs(seed: int = 0, part: int = 0) -> dict:
    key_list = jax.random.split(jax.random.key(seed), 13)
    own_keys = jax.random.split(jax.random.fold_in(key_list[12], part), 13)
    return {
        "features": normal_values(own_keys[0], (FRAMES, MAP * MAP, C), 1.0, 6.0, ((0, 32),)),
        "query_frame": place_ends(jax.random.randint(own_keys[1], (TRACKS,), 0, FRAMES), jax.random.fold_in(own_keys[1], 1), 0, FRAMES - 1).astype(jnp.int32),
        "query_pos": place_ends(jax.random.randint(own_keys[2], (TRACKS,), 0, MAP * MAP), jax.random.fold_in(own_keys[2], 1), 0, (MAP * MAP) - 1).astype(jnp.int32),
        "frame_order": jax.random.permutation(own_keys[3], FRAMES).astype(jnp.int32),
        "conv1_weight": normal_values(key_list[4], (CH1, 9), 9 ** -0.5, 2.0, (), jnp.float32),
        "conv1_bias": jnp.clip(jax.random.uniform(key_list[5], (CH1,), jnp.float32, -0.5, 0.5), -0.5, 0.5),
        "conv2_weight": normal_values(key_list[6], (CH2, CH1, 2, 2), (CH1 * 4) ** -0.5, 0.75),
        "proj_weight": normal_values(key_list[7], (CH2 * GRID * GRID, P_SIZE), (CH2 * GRID * GRID) ** -0.5, 0.125),
        "norm_gains": jnp.clip(1.0 + 0.15 * jax.random.normal(key_list[8], (BLOCKS, 2, P_SIZE), jnp.float32), 0.25, 1.75),
        "time_kernels": normal_values(key_list[9], (BLOCKS, 3, P_SIZE), 0.5, 3.0, (), jnp.float32),
        "mix_up": normal_values(key_list[10], (BLOCKS, P_SIZE, HID), P_SIZE ** -0.5, 0.25),
        "mix_down": normal_values(key_list[11], (BLOCKS, HID, P_SIZE), HID ** -0.5, 0.125),
    }


def layer_norm(values):
    center = values - lax.optimization_barrier(jnp.mean(values, axis=-1, keepdims=True))
    spread = lax.optimization_barrier(jnp.mean(center * center, axis=-1, keepdims=True))
    return center * lax.rsqrt(spread + 1e-05)

def frame_rows(feature_map, queries, conv1_weight, conv1_bias, conv2_weight, proj_weight):
    channels = feature_map.shape[1]
    count = queries.shape[0]
    corr = jnp.dot(feature_map, queries.T, preferred_element_type=jnp.float32) / jnp.sqrt(jnp.float32(channels))
    cube = corr.reshape(MAP, MAP, count)
    padded = jnp.pad(cube, ((1, 1), (1, 1), (0, 0)))
    total = jnp.zeros((CH1, MAP, MAP, count), jnp.float32) + conv1_bias[:, None, None, None]
    for shift_y in range(3):
        for shift_x in range(3):
            window = padded[shift_y:shift_y + MAP, shift_x:shift_x + MAP, :]
            total = total + conv1_weight[:, 3 * shift_y + shift_x][:, None, None, None] * window[None]
    first = jax.nn.relu(total).astype(jnp.bfloat16)
    half = MAP // 2
    blocks = first.reshape(CH1, half, 2, half, 2, count).astype(jnp.float32)
    second = jnp.einsum('cyaxbt,ocab->oyxt', blocks, conv2_weight.astype(jnp.float32))
    second = jax.nn.relu(second)
    width = half // GRID
    pooled = second.reshape(CH2, GRID, width, GRID, width, count).mean(axis=(2, 4))
    pooled = pooled.reshape(CH2 * GRID * GRID, count).astype(jnp.bfloat16)
    rows = lax.dot_general(pooled, proj_weight, (((0,), (0,)), ((), ())), preferred_element_type=jnp.float32)
    return rows.astype(jnp.bfloat16)

def mix_tracks(rows, frame_order, norm_gains, time_kernels, mix_up, mix_down):
    total_frames = rows.shape[0]
    inverse = jnp.zeros((total_frames,), jnp.int32).at[frame_order].set(jnp.arange(total_frames, dtype=jnp.int32))
    state = rows[inverse].astype(jnp.float32)
    width = state.shape[-1]
    for block in range(norm_gains.shape[0]):
        normed = layer_norm(state) * norm_gains[block, 0]
        padded = jnp.pad(normed, ((1, 1), (0, 0), (0, 0)))
        state = state + time_kernels[block, 0] * padded[:-2] + time_kernels[block, 1] * padded[1:-1] + time_kernels[block, 2] * padded[2:]
        inner = (layer_norm(state) * norm_gains[block, 1]).astype(jnp.bfloat16).reshape(-1, width)
        hidden = jax.nn.gelu(jnp.dot(inner, mix_up[block], preferred_element_type=jnp.float32)).astype(jnp.bfloat16)
        state = state + jnp.dot(hidden, mix_down[block], preferred_element_type=jnp.float32).reshape(state.shape)
    return state[frame_order].astype(jnp.bfloat16)

def reference(features, query_frame, query_pos, frame_order, conv1_weight, conv1_bias, conv2_weight, proj_weight, norm_gains, time_kernels, mix_up, mix_down):
    queries = features[query_frame, query_pos]

    def one_frame(feature_map):
        return frame_rows(feature_map, queries, conv1_weight, conv1_bias, conv2_weight, proj_weight)
    rows = lax.map(one_frame, features)
    return mix_tracks(rows, frame_order, norm_gains, time_kernels, mix_up, mix_down)
```

```python
import functools
import math

import jax
import jax.numpy as jnp
from jax import lax
from jax.experimental import pallas as pl
from jax.experimental.pallas import tpu as pltpu
from jax.sharding import PartitionSpec as P

F32 = jnp.float32
BF16 = jnp.bfloat16
MESH = pl.DeviceIdType.MESH
LANES = 128


def iota(shape, axis):
    return lax.broadcasted_iota(jnp.int32, shape, axis)


def one_hot(mask):
    return jnp.where(mask, F32(1.0), F32(0.0)).astype(BF16)


def mm(a, b):
    return jnp.dot(a, b, preferred_element_type=F32)


def mm_nt(a, b):
    return lax.dot_general(a, b, (((1,), (1,)), ((), ())), preferred_element_type=F32)


def norm(values):
    center = values - jnp.mean(values, axis=-1, keepdims=True)
    spread = jnp.mean(center * center, axis=-1, keepdims=True)
    return center * lax.rsqrt(spread + 1e-05)


def send_to(target, me, source, recv, send_sem, recv_sem):
    pltpu.make_async_remote_copy(
        src_ref=source(target),
        dst_ref=recv.at[me],
        send_sem=send_sem,
        recv_sem=recv_sem,
        device_id={"frames": target},
        device_id_type=MESH,
    ).start()


def send_far_first(me, low, high, *copy, skip=0):
    def step(s, carry):
        target = lax.bitwise_xor(me, high - 1 - s)

        @pl.when(target >= skip)
        def _():
            send_to(target, me, *copy)

        return carry

    lax.fori_loop(0, high - low, step, 0)


def send_all(me, n, *copy):
    send_far_first(me, 1, n, *copy)


def send_all_ends_first(me, n, first, *copy):
    for target in range(first):

        @pl.when(me != target)
        def _():
            send_to(target, me, *copy)

    send_far_first(me, 1, n, *copy, skip=first)


def wait_bytes(n, ref, sem):
    part = ref.at[pl.ds(0, n - 1)]
    pltpu.make_async_copy(part, part, sem).wait()


def kernel(
    n,
    side,
    grid,
    frame_hbm,
    pos_hbm,
    order_hbm,
    w1_hbm,
    b1_hbm,
    w2_hbm,
    gains_hbm,
    taps_hbm,
    features_hbm,
    proj_hbm,
    up_hbm,
    down_hbm,
    out_ref,
    frame_ref,
    pos_ref,
    order_ref,
    w1_ref,
    b1_ref,
    w2_ref,
    gains_ref,
    taps_ref,
    feat,
    proj,
    up,
    down,
    proj_p,
    toeplitz,
    blocks,
    pacc,
    perm,
    perm_t,
    send1,
    recv1,
    send2,
    recv2,
    send3,
    recv3,
    send4,
    recv4,
    local_sem,
    send_sem,
    recv_sem,
):
    me = lax.axis_index("frames")
    positions, channels = feat.shape
    tracks = pos_ref.shape[1]
    per = tracks // n
    ch1 = w1_ref.shape[0]
    ch2 = w2_ref.shape[1]
    width = proj.shape[1]
    hid = up.shape[2]
    qc = channels // LANES
    wc = width // LANES
    half = side // 2
    pool = half // grid
    row_blocks = positions // LANES

    small = [
        pltpu.make_async_copy(source, target, local_sem.at[4 + i])
        for i, (source, target) in enumerate(
            (
                (frame_hbm, frame_ref),
                (pos_hbm, pos_ref),
                (w1_hbm, w1_ref),
                (b1_hbm, b1_ref),
                (w2_hbm, w2_ref),
                (order_hbm, order_ref),
                (gains_hbm, gains_ref),
                (taps_hbm, taps_ref),
            )
        )
    ]
    small[0].start()
    small[1].start()
    copy_f = pltpu.make_async_copy(features_hbm, feat, local_sem.at[0])
    copy_f.start()

    barrier = pltpu.get_barrier_semaphore()

    def greet(s, carry):
        pl.semaphore_signal(
            barrier, inc=1, device_id={"frames": lax.rem(me + s, n)}, device_id_type=MESH
        )
        return carry

    lax.fori_loop(1, n, greet, 0)

    for copy in small[2:]:
        copy.start()
    small[0].wait()
    small[1].wait()
    key = jnp.where(frame_ref[...] == me, pos_ref[...], -1).astype(F32)
    key_col = jnp.transpose(jnp.broadcast_to(key, (tracks, tracks)))[:, :1].astype(jnp.int32)
    copy_f.wait()
    copy_p = pltpu.make_async_copy(proj_hbm, proj, local_sem.at[1])
    copy_u = pltpu.make_async_copy(up_hbm, up, local_sem.at[2])
    copy_d = pltpu.make_async_copy(down_hbm, down, local_sem.at[3])
    copy_p.start()
    copy_u.start()
    copy_d.start()
    picked = jnp.zeros((tracks, channels), F32)
    chunk = 1024
    for start in range(0, positions, chunk):
        chosen = one_hot(iota((tracks, chunk), 1) + start == key_col)
        picked = picked + mm(chosen, feat[start : start + chunk, :])
    picked = picked.astype(BF16)
    stacked = jnp.concatenate(
        [picked[:, c * LANES : (c + 1) * LANES] for c in range(qc)], axis=0
    )
    def spread_rows(count):
        rows = n * count * per
        r = iota((rows, count * tracks), 0)
        s = iota((rows, count * tracks), 1)
        source = ((r // per) % count) * tracks + (r // (per * count)) * per + r % per
        return one_hot(source == s)

    def gather_rows(count, c):
        r = iota((tracks, n * count * per), 0)
        s = iota((tracks, n * count * per), 1)
        source = (r // per) * (count * per) + c * per + r % per
        return one_hot(source == s)

    spread1 = mm(spread_rows(qc), stacked)
    send1[...] = spread1.reshape(n, qc * per, LANES).astype(BF16)
    pl.semaphore_wait(barrier, n - 1)
    send_all(me, n, lambda t: send1.at[t], recv1, send_sem.at[0], recv_sem.at[0])
    recv1[me] = send1[me]

    for copy in small[2:]:
        copy.wait()
    lane = iota((1, LANES), 1)
    lane_k = lane % ch1
    taps = []
    for tap in range(9):
        vec = jnp.zeros((1, LANES), F32)
        for k in range(ch1):
            vec = jnp.where(lane_k == k, w1_ref[k, tap], vec)
        taps.append(vec)
    bias = jnp.zeros((1, LANES), F32)
    for k in range(ch1):
        bias = jnp.where(lane_k == k, b1_ref[k], bias)
    cells = LANES // ch2
    halves = grid // cells
    groups = halves * pool
    for g in range(groups):
        h, e = g // pool, g % pool
        x_out = (
            (cells * h + lane // (2 * ch1)) * (2 * pool) + 2 * e + (lane // ch1) % 2
        )
        dx = iota((side, LANES), 0) - x_out + 1
        bands = []
        for dy in range(3):
            band = jnp.where(dx == 0, taps[3 * dy], F32(0.0))
            band = jnp.where(dx == 1, taps[3 * dy + 1], band)
            band = jnp.where(dx == 2, taps[3 * dy + 2], band)
            bands.append(band.astype(BF16))
        zero = jnp.zeros((side, LANES), BF16)
        for r in range(4):
            for a in range(2):
                dy = r - a
                toeplitz[g, r * side : (r + 1) * side, a * LANES : (a + 1) * LANES] = (
                    bands[dy] if 0 <= dy < 3 else zero
                )
    wait_bytes(n, recv1, recv_sem.at[0])
    mine = jnp.sum(recv1[...].astype(F32), axis=0)
    send2[...] = mine.astype(BF16)
    send_all(me, n, lambda t: send2, recv2, send_sem.at[1], recv_sem.at[1])
    recv2[me] = send2[...]

    r = iota((2 * LANES, 4 * ch1), 0)
    s = iota((2 * LANES, 4 * ch1), 1)
    select = one_hot(s == (r % ch1) * 4 + (1 - r // LANES) * 2 + (r // ch1) % 2)
    c_lane = iota((LANES, ch2), 0)
    expand = one_hot(
        iota((LANES, ch2), 1) == (c_lane // (cells * 4)) * 4 + c_lane % 4
    )
    taps2 = mm_nt(mm(select, w2_ref[...]).astype(BF16), expand)
    r = iota((2 * LANES, LANES), 0)
    c = iota((2 * LANES, LANES), 1)
    conv2 = jnp.where((r // (2 * ch1)) % cells == (c // 4) % cells, taps2, 0.0).astype(BF16)

    window_count = grid * grid
    rows = 4 * window_count
    r = iota((rows, rows), 0)
    s = iota((rows, rows), 1)
    reorder = one_hot(s == (r % 4) * window_count + r // 4)
    copy_p.wait()
    for b in range(ch2 // 4):
        moved = mm(reorder, proj[b * rows : (b + 1) * rows, :])
        proj_p[:, b] = moved.astype(BF16).reshape(grid * halves, cells * 4, width)

    col = iota((1, n * wc * per), 1)
    order = jnp.zeros((1, n * wc * per), jnp.int32)
    for f in range(n):
        order = jnp.where(col // (wc * per) == f, order_ref[f], order)
    for c in range(wc):
        want = jnp.where((col // per) % wc == c, order * per + col % per, -1)
        hot = jnp.where(
            iota((n * per, n * wc * per), 0) == want, F32(1.0), F32(0.0)
        )
        perm[c] = hot.astype(BF16)
        perm_t[c] = jnp.transpose(hot).astype(BF16)

    blocks[0] = jnp.zeros((tracks, LANES), BF16)
    blocks[row_blocks + 1] = jnp.zeros((tracks, LANES), BF16)

    wait_bytes(n, recv2, recv_sem.at[1])
    got = recv2[...].astype(F32).reshape(n * qc * per, LANES).astype(BF16)
    scale = 1.0 / math.sqrt(channels)
    queries = jnp.concatenate([mm(gather_rows(qc, c), got) for c in range(qc)], axis=1)
    queries = (queries * scale).astype(BF16)

    for start in range(0, positions, chunk):
        corr = mm_nt(queries, feat[start : start + chunk, :]).astype(BF16)
        for j in range(chunk // LANES):
            blocks[1 + start // LANES + j] = corr[:, j * LANES : (j + 1) * LANES]

    bias2 = jnp.concatenate([bias, bias], axis=1)

    def first_rows(start, count, band):
        left = blocks[pl.ds(start, count)].reshape(count * tracks, LANES)
        right = blocks[pl.ds(start + 1, count)].reshape(count * tracks, LANES)
        total = mm(jnp.concatenate([left, right], axis=1), band) + bias2
        return jnp.maximum(total, 0.0).astype(BF16)

    pacc[...] = jnp.zeros_like(pacc)

    def group(g, carry):
        band = toeplitz[g]
        h = g // pool
        before = first_rows(0, 1, band)[:, LANES:]

        def window(i, before):
            first = first_rows(1 + i * pool, pool, band)
            lower = first[:, :LANES]
            upper = jnp.concatenate([before, first[: (pool - 1) * tracks, LANES:]], axis=0)
            second = mm(jnp.concatenate([lower, upper], axis=1), conv2)
            second = jnp.maximum(second, 0.0).reshape(pool, tracks, LANES)
            pacc[i * halves + h] += jnp.sum(second, axis=0)
            return first[(pool - 1) * tracks :, LANES:]

        lax.fori_loop(0, grid, window, before, unroll=8)
        return carry

    lax.fori_loop(0, groups, group, 0, unroll=2)

    area = pool * pool
    pooled = jnp.concatenate(
        [(pacc[j] * (1.0 / area)).astype(BF16) for j in range(grid * halves)], axis=1
    )
    frame_rows = mm(pooled, proj_p[...].reshape(pooled.shape[1], width)).astype(BF16)
    stacked = jnp.concatenate(
        [frame_rows[:, c * LANES : (c + 1) * LANES] for c in range(wc)], axis=0
    )
    send3[...] = mm(spread_rows(wc), stacked).reshape(n, wc * per, LANES).astype(BF16)
    send_all(me, n, lambda t: send3.at[t], recv3, send_sem.at[2], recv_sem.at[2])
    recv3[me] = send3[me]
    copy_u.wait()
    copy_d.wait()
    wait_bytes(n, recv3, recv_sem.at[2])
    got = recv3[...].reshape(n * wc * per, LANES)
    state = jnp.concatenate([mm(perm[c], got) for c in range(wc)], axis=1)
    row = iota((n * per, 1), 0)
    for block in range(up.shape[0]):
        normed = norm(state) * gains_ref[block, 0:1, :]
        earlier = jnp.where(row >= per, pltpu.roll(normed, per, 0), 0.0)
        later = jnp.where(row < (n - 1) * per, pltpu.roll(normed, (n - 1) * per, 0), 0.0)
        state = (
            state
            + taps_ref[0, pl.ds(block, 1), :] * earlier
            + taps_ref[1, pl.ds(block, 1), :] * normed
            + taps_ref[2, pl.ds(block, 1), :] * later
        )
        inner = (norm(state) * gains_ref[block, 1:2, :]).astype(BF16)
        step = 512
        for start in range(0, hid, step):
            hidden = jax.nn.gelu(mm(inner, up[block, :, start : start + step])).astype(BF16)
            state = state + mm(hidden, down[block, start : start + step, :])
    result = state.astype(BF16)
    back = mm(perm_t[0], result[:, :LANES])
    for c in range(1, wc):
        back = back + mm(perm_t[c], result[:, c * LANES : (c + 1) * LANES])
    send4[...] = back.reshape(n, wc * per, LANES).astype(BF16)
    send_all_ends_first(me, n, 2, lambda t: send4.at[t], recv4, send_sem.at[3], recv_sem.at[3])
    recv4[me] = send4[me]
    wait_bytes(n, recv4, recv_sem.at[3])
    got = recv4[...].reshape(n * wc * per, LANES)
    for c in range(wc):
        out_ref[:, c * LANES : (c + 1) * LANES] = mm(gather_rows(wc, c), got).astype(BF16)
    wait_bytes(n, recv1, send_sem.at[0])
    wait_bytes(n, recv2, send_sem.at[1])
    wait_bytes(n, recv3, send_sem.at[2])
    wait_bytes(n, recv4, send_sem.at[3])


def on_device(
    features,
    query_frame,
    query_pos,
    frame_order,
    conv1_weight,
    conv1_bias,
    conv2_weight,
    proj_weight,
    norm_gains,
    time_kernels,
    mix_up,
    mix_down,
):
    n = lax.axis_size("frames")
    _, positions, channels = features.shape
    tracks = query_frame.shape[0]
    per = tracks // n
    width = proj_weight.shape[1]
    ch2, ch1 = conv2_weight.shape[:2]
    side = math.isqrt(positions)
    grid = math.isqrt(proj_weight.shape[0] // ch2)
    qc, wc = channels // LANES, width // LANES
    cells = LANES // ch2
    halves = grid // cells
    groups = halves * (side // 2 // grid)
    vmem = pl.BlockSpec(memory_space=pltpu.VMEM)
    hbm = pl.BlockSpec(memory_space=pltpu.HBM)
    out = pl.pallas_call(
        functools.partial(kernel, n, side, grid),
        out_shape=pltpu.VMEM((tracks, width), BF16),
        in_specs=[hbm] * 12,
        out_specs=vmem,
        scratch_shapes=[
            pltpu.VMEM((1, tracks), jnp.int32),
            pltpu.VMEM((1, tracks), jnp.int32),
            pltpu.SMEM(frame_order.shape, jnp.int32),
            pltpu.SMEM(conv1_weight.shape, F32),
            pltpu.SMEM(conv1_bias.shape, F32),
            pltpu.VMEM((ch1 * 4, ch2), BF16),
            pltpu.VMEM(norm_gains.shape, F32),
            pltpu.VMEM((3, norm_gains.shape[0], width), F32),
            pltpu.VMEM((positions, channels), BF16),
            pltpu.VMEM(proj_weight.shape, BF16),
            pltpu.VMEM(mix_up.shape, BF16),
            pltpu.VMEM(mix_down.shape, BF16),
            pltpu.VMEM((grid * halves, ch2 // 4, cells * 4, width), BF16),
            pltpu.VMEM((groups, 4 * side, 2 * LANES), BF16),
            pltpu.VMEM((positions // LANES + 2, tracks, LANES), BF16),
            pltpu.VMEM((grid * halves, tracks, LANES), F32),
            pltpu.VMEM((wc, tracks, n * wc * per), BF16),
            pltpu.VMEM((wc, n * wc * per, tracks), BF16),
            pltpu.VMEM((n, qc * per, LANES), BF16),
            pltpu.VMEM((n, qc * per, LANES), BF16),
            pltpu.VMEM((qc * per, LANES), BF16),
            pltpu.VMEM((n, qc * per, LANES), BF16),
            pltpu.VMEM((n, wc * per, LANES), BF16),
            pltpu.VMEM((n, wc * per, LANES), BF16),
            pltpu.VMEM((n, wc * per, LANES), BF16),
            pltpu.VMEM((n, wc * per, LANES), BF16),
            pltpu.SemaphoreType.DMA((12,)),
            pltpu.SemaphoreType.DMA((4,)),
            pltpu.SemaphoreType.DMA((4,)),
        ],
        compiler_params=pltpu.CompilerParams(
            collective_id=0, has_side_effects=True, vmem_limit_bytes=56 * 1024 * 1024
        ),
    )(
        query_frame.reshape(1, tracks),
        query_pos.reshape(1, tracks),
        frame_order,
        conv1_weight,
        conv1_bias,
        conv2_weight.transpose(1, 2, 3, 0).reshape(ch1 * 4, ch2),
        norm_gains,
        time_kernels.transpose(1, 0, 2),
        features.reshape(positions, channels),
        proj_weight,
        mix_up,
        mix_down,
    )
    return out[None]


def solution(mesh):
    placed = (
        P(("groups", "frames"), None, None),
        P("groups"),
        P("groups"),
        P("groups"),
        P(),
        P(),
        P(),
        P(),
        P(),
        P(),
        P(),
        P(),
    )
    return jax.shard_map(
        on_device,
        mesh=mesh,
        in_specs=placed,
        out_specs=P(("groups", "frames"), None, None),
        check_vma=False,
    )
```

```python
import functools
import math

import jax
import jax.numpy as jnp
from jax import lax
from jax.experimental import pallas as pl
from jax.experimental.pallas import tpu as pltpu
from jax.sharding import PartitionSpec as P

F32 = jnp.float32
BF16 = jnp.bfloat16
MESH = pl.DeviceIdType.MESH
LANES = 128


def iota(shape, axis):
    return lax.broadcasted_iota(jnp.int32, shape, axis)


def one_hot(mask):
    return jnp.where(mask, F32(1.0), F32(0.0)).astype(BF16)


def mm(a, b):
    return jnp.dot(a, b, preferred_element_type=F32)


def mm_nt(a, b):
    return lax.dot_general(a, b, (((1,), (1,)), ((), ())), preferred_element_type=F32)


def norm(values):
    center = values - jnp.mean(values, axis=-1, keepdims=True)
    spread = jnp.mean(center * center, axis=-1, keepdims=True)
    return center * lax.rsqrt(spread + 1e-05)


def send_to(target, me, source, recv, send_sem, recv_sem):
    pltpu.make_async_remote_copy(
        src_ref=source(target),
        dst_ref=recv.at[me],
        send_sem=send_sem,
        recv_sem=recv_sem,
        device_id={"frames": target},
        device_id_type=MESH,
    ).start()


def send_far_first(me, low, high, *copy, skip=0):
    def step(s, carry):
        target = lax.bitwise_xor(me, high - 1 - s)

        @pl.when(target >= skip)
        def _():
            send_to(target, me, *copy)

        return carry

    lax.fori_loop(0, high - low, step, 0)


def send_all(me, n, *copy):
    send_far_first(me, 1, n, *copy)


def send_all_ends_first(me, n, first, *copy):
    for target in range(first):

        @pl.when(me != target)
        def _():
            send_to(target, me, *copy)

    send_far_first(me, 1, n, *copy, skip=first)


def wait_messages(count, ref, sem):
    part = ref.at[pl.ds(0, count)]
    pltpu.make_async_copy(part, part, sem).wait()


def kernel(
    n,
    side,
    grid,
    frame_hbm,
    pos_hbm,
    order_hbm,
    w1_hbm,
    b1_hbm,
    w2_hbm,
    gains_hbm,
    taps_hbm,
    features_hbm,
    proj_hbm,
    up_hbm,
    down_hbm,
    out_ref,
    frame_ref,
    pos_ref,
    order_ref,
    w1_ref,
    b1_ref,
    w2_ref,
    gains_ref,
    taps_ref,
    feat,
    proj,
    up,
    down,
    proj_p,
    toeplitz,
    blocks,
    pacc,
    links,
    send1,
    recv1,
    send2,
    recv2,
    send3,
    recv3,
    send4,
    recv4,
    local_sem,
    feat_sem,
    send_sem,
    recv_sem,
):
    me = lax.axis_index("frames")
    positions, channels = side * side, feat.shape[1]
    tracks = pos_ref.shape[1]
    per = tracks // n
    ch1 = w1_ref.shape[0]
    ch2 = w2_ref.shape[1]
    width = proj.shape[1]
    hid = up.shape[2]
    qc = channels // LANES
    wc = width // LANES
    half = side // 2
    pool = half // grid
    share = n // 2
    part = tracks // 2
    near = (me // share) * share
    far = share - near

    small = [
        pltpu.make_async_copy(source, target, local_sem.at[4 + i])
        for i, (source, target) in enumerate(
            (
                (frame_hbm, frame_ref),
                (pos_hbm, pos_ref),
                (w1_hbm, w1_ref),
                (b1_hbm, b1_ref),
                (w2_hbm, w2_ref),
                (order_hbm, order_ref),
                (gains_hbm, gains_ref),
                (taps_hbm, taps_ref),
            )
        )
    ]
    small[0].start()
    small[1].start()
    chunk = 1024
    copies = [
        pltpu.make_async_copy(
            features_hbm.at[pl.ds(start, chunk)],
            feat.at[pl.ds(side + start, chunk)],
            feat_sem.at[start // chunk],
        )
        for start in range(0, positions, chunk)
    ]
    for copy in copies:
        copy.start()

    barrier = pltpu.get_barrier_semaphore()

    def greet(s, carry):
        pl.semaphore_signal(
            barrier, inc=1, device_id={"frames": lax.rem(me + s, n)}, device_id_type=MESH
        )
        return carry

    lax.fori_loop(1, n, greet, 0)

    for copy in small[2:]:
        copy.start()
    small[0].wait()
    small[1].wait()
    key = jnp.where(frame_ref[...] == me, pos_ref[...], -1).astype(F32)
    key_col = jnp.transpose(jnp.broadcast_to(key, (tracks, tracks)))[:, :1].astype(jnp.int32)
    picked = jnp.zeros((tracks, channels), F32)
    for copy, start in zip(copies, range(0, positions, chunk)):
        chosen = one_hot(iota((tracks, chunk), 1) + start == key_col)
        copy.wait()
        picked = picked + mm(chosen, feat[side + start : side + start + chunk, :])
    copy_p = pltpu.make_async_copy(proj_hbm, proj, local_sem.at[1])
    copy_u = pltpu.make_async_copy(up_hbm, up, local_sem.at[2])
    copy_d = pltpu.make_async_copy(down_hbm, down, local_sem.at[3])
    copy_p.start()
    copy_u.start()
    copy_d.start()
    picked = picked.astype(BF16)
    stacked = jnp.concatenate(
        [picked[:, c * LANES : (c + 1) * LANES] for c in range(qc)], axis=0
    )

    def spread_rows(count, owners):
        rows = owners * count * per
        r = iota((rows, rows), 0)
        s = iota((rows, rows), 1)
        source = (
            ((r // per) % count) * owners * per + (r // (per * count)) * per + r % per
        )
        return one_hot(source == s)

    def gather_rows(count, c, owners, turn=0):
        r = iota((owners * per, owners * count * per), 0)
        s = iota((owners * per, owners * count * per), 1)
        source = ((r // per + turn) % owners) * (count * per) + c * per + r % per
        return one_hot(source == s)

    spread1 = mm(spread_rows(qc, n), stacked)
    send1[...] = spread1.reshape(n, qc * per, LANES).astype(BF16)
    pl.semaphore_wait(barrier, n - 1)
    send_all(me, n, lambda t: send1.at[t], recv1, send_sem.at[0], recv_sem.at[0])
    recv1[me] = send1[me]

    for copy in small[2:]:
        copy.wait()
    lane = iota((1, LANES), 1)
    lane_k = lane % ch1
    taps = []
    for tap in range(9):
        vec = jnp.zeros((1, LANES), F32)
        for k in range(ch1):
            vec = jnp.where(lane_k == k, w1_ref[k, tap], vec)
        taps.append(vec)
    bias = jnp.zeros((1, LANES), F32)
    for k in range(ch1):
        bias = jnp.where(lane_k == k, b1_ref[k], bias)
    cells = LANES // ch2
    halves = grid // cells
    groups = halves * pool
    for g in range(groups):
        h, e = g // pool, g % pool
        x_out = (
            (cells * h + lane // (2 * ch1)) * (2 * pool) + 2 * e + (lane // ch1) % 2
        )
        dx = iota((side, LANES), 0) - x_out + 1
        bands = []
        for dy in range(3):
            band = jnp.where(dx == 0, taps[3 * dy], F32(0.0))
            band = jnp.where(dx == 1, taps[3 * dy + 1], band)
            band = jnp.where(dx == 2, taps[3 * dy + 2], band)
            bands.append(band.astype(BF16))
        zero = jnp.zeros((side, LANES), BF16)
        for r in range(4):
            for a in range(2):
                dy = r - a
                toeplitz[g, r * side : (r + 1) * side, a * LANES : (a + 1) * LANES] = (
                    bands[dy] if 0 <= dy < 3 else zero
                )
    wait_messages(n - 1, recv1, recv_sem.at[0])
    mine = jnp.sum(recv1[...].astype(F32), axis=0)
    send2[...] = mine.astype(BF16)
    send_far_first(me, 1, share, lambda t: send2, recv2, send_sem.at[1], recv_sem.at[1])
    send_far_first(me, share, n, lambda t: send2, recv2, send_sem.at[1], recv_sem.at[4])
    recv2[me] = send2[...]

    r = iota((2 * LANES, 4 * ch1), 0)
    s = iota((2 * LANES, 4 * ch1), 1)
    select = one_hot(s == (r % ch1) * 4 + (r // LANES) * 2 + (r // ch1) % 2)
    c_lane = iota((LANES, ch2), 0)
    expand = one_hot(
        iota((LANES, ch2), 1) == (c_lane // (cells * 4)) * 4 + c_lane % 4
    )
    taps2 = mm_nt(mm(select, w2_ref[...]).astype(BF16), expand)
    r = iota((2 * LANES, LANES), 0)
    c = iota((2 * LANES, LANES), 1)
    conv2 = jnp.where((r // (2 * ch1)) % cells == (c // 4) % cells, taps2, 0.0).astype(BF16)

    window_count = grid * grid
    rows = 4 * window_count
    r = iota((rows, rows), 0)
    s = iota((rows, rows), 1)
    reorder = one_hot(s == (r % 4) * window_count + r // 4)
    copy_p.wait()
    for b in range(ch2 // 4):
        moved = mm(reorder, proj[b * rows : (b + 1) * rows, :])
        proj_p[:, b] = moved.astype(BF16).reshape(grid * halves, cells * 4, width)

    rows = n * per
    lane_row = iota((1, rows), 1)
    order = jnp.zeros((1, rows), jnp.int32)
    for f in range(n):
        order = jnp.where(lane_row // per == f, order_ref[f], order)
    place = (order * per + lane_row % per).astype(F32)
    place_col = jnp.transpose(jnp.broadcast_to(place, (rows, rows)))
    earlier_hot = one_hot(place_col - per == place)
    later_hot = one_hot(place_col + per == place)
    links[...] = jnp.concatenate(
        [
            jnp.concatenate([earlier_hot, earlier_hot], axis=1),
            jnp.concatenate([later_hot, later_hot], axis=1),
        ],
        axis=0,
    )

    feat[:side, :] = jnp.zeros((side, channels), BF16)
    feat[side + positions :, :] = jnp.zeros((side, channels), BF16)

    scale = 1.0 / math.sqrt(channels)
    bias2 = jnp.concatenate([bias, bias], axis=1)
    area = pool * pool
    span = 2

    def frame_part(c, owners):
        got = recv2[pl.ds(owners, share)].astype(F32)
        got = got.reshape(share * qc * per, LANES).astype(BF16)
        queries = jnp.concatenate(
            [mm(gather_rows(qc, k, share), got) for k in range(qc)], axis=1
        )
        queries = (queries * scale).astype(BF16)
        for start in range(0, positions + LANES, chunk):
            size = min(chunk, positions + LANES - start)
            corr = mm_nt(queries, feat[start : start + size, :]).astype(BF16)
            for j in range(size // LANES):
                blocks[c, start // LANES + j] = corr[:, j * LANES : (j + 1) * LANES]

        pacc[...] = jnp.zeros_like(pacc)
        count = span * pool

        def group(g, carry):
            band = toeplitz[g]
            h = g // pool

            def window(i, carry):
                above = blocks[c, pl.ds(i * count, count)].reshape(count * part, LANES)
                below = blocks[c, pl.ds(i * count + 1, count)].reshape(count * part, LANES)
                first = mm(jnp.concatenate([above, below], axis=1), band) + bias2
                first = jnp.maximum(first.astype(BF16), BF16(0))
                second = jnp.maximum(mm(first, conv2), 0.0)
                second = second.reshape(span, pool, part, LANES)
                for u in range(span):
                    pacc[(i * span + u) * halves + h] += jnp.sum(second[u], axis=0)
                return carry

            return lax.fori_loop(0, grid // span, window, carry, unroll=True)

        lax.fori_loop(0, groups, group, 0, unroll=4)
        pooled = jnp.concatenate(
            [(pacc[j] * (1.0 / area)).astype(BF16) for j in range(grid * halves)], axis=1
        )
        frame_rows = mm(pooled, proj_p[...].reshape(pooled.shape[1], width)).astype(BF16)
        stacked = jnp.concatenate(
            [frame_rows[:, k * LANES : (k + 1) * LANES] for k in range(wc)], axis=0
        )
        spread = mm(spread_rows(wc, share), stacked).astype(BF16)
        send3[pl.ds(share - owners, share)] = spread.reshape(share, wc * per, LANES)

    wait_messages(share - 1, recv2, recv_sem.at[1])
    frame_part(0, near)
    send_far_first(
        me, share, n, lambda t: send3.at[t], recv3, send_sem.at[2], recv_sem.at[2]
    )
    wait_messages(share, recv2, recv_sem.at[4])
    frame_part(1, far)
    send_far_first(
        me, 1, share, lambda t: send3.at[t], recv3, send_sem.at[2], recv_sem.at[2]
    )
    recv3[me] = send3[me]
    copy_u.wait()
    copy_d.wait()
    wait_messages(n - 1, recv3, recv_sem.at[2])
    got = recv3[...].reshape(n * wc * per, LANES)
    state = jnp.concatenate([mm(gather_rows(wc, c, n), got) for c in range(wc)], axis=1)
    for block in range(up.shape[0]):
        normed = norm(state) * gains_ref[block, 0:1, :]
        high = normed.astype(BF16)
        low = (normed - high.astype(F32)).astype(BF16)
        moved = mm(links[...], jnp.concatenate([high, low], axis=0))
        earlier, later = moved[: n * per], moved[n * per :]
        state = (
            state
            + taps_ref[0, pl.ds(block, 1), :] * earlier
            + taps_ref[1, pl.ds(block, 1), :] * normed
            + taps_ref[2, pl.ds(block, 1), :] * later
        )
        inner = (norm(state) * gains_ref[block, 1:2, :]).astype(BF16)
        hidden = jax.nn.gelu(mm(inner, up[block])).astype(BF16)
        state = state + mm(hidden, down[block])
    result = state.astype(BF16)
    stacked = jnp.concatenate(
        [result[:, c * LANES : (c + 1) * LANES] for c in range(wc)], axis=0
    )
    back = mm(spread_rows(wc, n), stacked)
    send4[...] = back.reshape(n, wc * per, LANES).astype(BF16)
    send_all_ends_first(me, n, 2, lambda t: send4.at[t], recv4, send_sem.at[3], recv_sem.at[3])
    recv4[me] = send4[me]
    wait_messages(n - 1, recv4, recv_sem.at[3])
    got = recv4[...].reshape(n * wc * per, LANES)
    for c in range(wc):
        out_ref[:, c * LANES : (c + 1) * LANES] = mm(
            gather_rows(wc, c, n, share), got
        ).astype(BF16)
    wait_messages(n - 1, recv1, send_sem.at[0])
    wait_messages(n - 1, recv2, send_sem.at[1])
    wait_messages(n - 1, recv3, send_sem.at[2])
    wait_messages(n - 1, recv4, send_sem.at[3])


def on_device(
    features,
    query_frame,
    query_pos,
    frame_order,
    conv1_weight,
    conv1_bias,
    conv2_weight,
    proj_weight,
    norm_gains,
    time_kernels,
    mix_up,
    mix_down,
):
    n = lax.axis_size("frames")
    _, positions, channels = features.shape
    tracks = query_frame.shape[0]
    per = tracks // n
    width = proj_weight.shape[1]
    ch2, ch1 = conv2_weight.shape[:2]
    side = math.isqrt(positions)
    grid = math.isqrt(proj_weight.shape[0] // ch2)
    qc, wc = channels // LANES, width // LANES
    cells = LANES // ch2
    halves = grid // cells
    groups = halves * (side // 2 // grid)
    vmem = pl.BlockSpec(memory_space=pltpu.VMEM)
    hbm = pl.BlockSpec(memory_space=pltpu.HBM)
    out = pl.pallas_call(
        functools.partial(kernel, n, side, grid),
        out_shape=pltpu.VMEM((tracks, width), BF16),
        in_specs=[hbm] * 12,
        out_specs=vmem,
        scratch_shapes=[
            pltpu.VMEM((1, tracks), jnp.int32),
            pltpu.VMEM((1, tracks), jnp.int32),
            pltpu.SMEM(frame_order.shape, jnp.int32),
            pltpu.SMEM(conv1_weight.shape, F32),
            pltpu.SMEM(conv1_bias.shape, F32),
            pltpu.VMEM((ch1 * 4, ch2), BF16),
            pltpu.VMEM(norm_gains.shape, F32),
            pltpu.VMEM((3, norm_gains.shape[0], width), F32),
            pltpu.VMEM((positions + 2 * side, channels), BF16),
            pltpu.VMEM(proj_weight.shape, BF16),
            pltpu.VMEM(mix_up.shape, BF16),
            pltpu.VMEM(mix_down.shape, BF16),
            pltpu.VMEM((grid * halves, ch2 // 4, cells * 4, width), BF16),
            pltpu.VMEM((groups, 4 * side, 2 * LANES), BF16),
            pltpu.VMEM((2, positions // LANES + 1, tracks // 2, LANES), BF16),
            pltpu.VMEM((grid * halves, tracks // 2, LANES), F32),
            pltpu.VMEM((2 * tracks, 2 * tracks), BF16),
            pltpu.VMEM((n, qc * per, LANES), BF16),
            pltpu.VMEM((n, qc * per, LANES), BF16),
            pltpu.VMEM((qc * per, LANES), BF16),
            pltpu.VMEM((n, qc * per, LANES), BF16),
            pltpu.VMEM((n, wc * per, LANES), BF16),
            pltpu.VMEM((n, wc * per, LANES), BF16),
            pltpu.VMEM((n, wc * per, LANES), BF16),
            pltpu.VMEM((n, wc * per, LANES), BF16),
            pltpu.SemaphoreType.DMA((12,)),
            pltpu.SemaphoreType.DMA((positions // 1024,)),
            pltpu.SemaphoreType.DMA((4,)),
            pltpu.SemaphoreType.DMA((5,)),
        ],
        compiler_params=pltpu.CompilerParams(
            collective_id=0, has_side_effects=True, vmem_limit_bytes=56 * 1024 * 1024
        ),
    )(
        query_frame.reshape(1, tracks),
        query_pos.reshape(1, tracks),
        frame_order,
        conv1_weight,
        conv1_bias,
        conv2_weight.transpose(1, 2, 3, 0).reshape(ch1 * 4, ch2),
        norm_gains,
        time_kernels.transpose(1, 0, 2),
        features.reshape(positions, channels),
        proj_weight,
        mix_up,
        mix_down,
    )
    return out[None]


def solution(mesh):
    placed = (
        P(("groups", "frames"), None, None),
        P("groups"),
        P("groups"),
        P("groups"),
        P(),
        P(),
        P(),
        P(),
        P(),
        P(),
        P(),
        P(),
    )
    return jax.shard_map(
        on_device,
        mesh=mesh,
        in_specs=placed,
        out_specs=P(("groups", "frames"), None, None),
        check_vma=False,
    )
```

```python
import functools
import math

import jax
import jax.numpy as jnp
from jax import lax
from jax.experimental import pallas as pl
from jax.experimental.pallas import tpu as pltpu
from jax.sharding import PartitionSpec as P

F32 = jnp.float32
BF16 = jnp.bfloat16
MESH = pl.DeviceIdType.MESH
LANES = 128


def iota(shape, axis):
    return lax.broadcasted_iota(jnp.int32, shape, axis)


def one_hot(mask):
    return jnp.where(mask, F32(1.0), F32(0.0)).astype(BF16)


def mm(a, b):
    return jnp.dot(a, b, preferred_element_type=F32)


def mm_nt(a, b):
    return lax.dot_general(a, b, (((1,), (1,)), ((), ())), preferred_element_type=F32)


def norm(values):
    center = values - jnp.mean(values, axis=-1, keepdims=True)
    spread = jnp.mean(center * center, axis=-1, keepdims=True)
    return center * lax.rsqrt(spread + 1e-05)


def send_far_first(me, low, high, source, recv, send_sem, recv_sem):
    def step(s, carry):
        target = lax.bitwise_xor(me, high - 1 - s)
        pltpu.make_async_remote_copy(
            src_ref=source(target),
            dst_ref=recv.at[me],
            send_sem=send_sem,
            recv_sem=recv_sem,
            device_id={"frames": target},
            device_id_type=MESH,
        ).start()
        return carry

    lax.fori_loop(0, high - low, step, 0, unroll=True)


def wait_messages(count, ref, sem):
    part = ref.at[pl.ds(0, count)]
    pltpu.make_async_copy(part, part, sem).wait()


def kernel(
    n,
    side,
    grid,
    frame_hbm,
    pos_hbm,
    order_hbm,
    w1_hbm,
    b1_hbm,
    w2_hbm,
    gains_hbm,
    taps_hbm,
    features_hbm,
    proj_hbm,
    up_hbm,
    down_hbm,
    out_ref,
    frame_ref,
    pos_ref,
    order_ref,
    w1_ref,
    b1_ref,
    w2_ref,
    gains_ref,
    taps_ref,
    feat,
    proj,
    up,
    down,
    proj_p,
    toeplitz,
    blocks,
    pacc,
    links,
    stage,
    send1,
    recv1,
    send2,
    recv2,
    send3,
    recv3,
    send4,
    recv4,
    local_sem,
    feat_sem,
    send_sem,
    recv_sem,
):
    me = lax.axis_index("frames")
    positions, channels = side * side, feat.shape[1]
    tracks = pos_ref.shape[1]
    per = tracks // n
    ch1 = w1_ref.shape[0]
    ch2 = w2_ref.shape[1]
    width = proj.shape[1]
    hid = up.shape[2]
    qc = channels // LANES
    wc = width // LANES
    half = side // 2
    pool = half // grid
    share = n // 2
    part = tracks // 2
    near = (me // share) * share
    far = share - near

    small = [
        pltpu.make_async_copy(source, target, local_sem.at[4 + i])
        for i, (source, target) in enumerate(
            (
                (frame_hbm, frame_ref),
                (pos_hbm, pos_ref),
                (w1_hbm, w1_ref),
                (b1_hbm, b1_ref),
                (w2_hbm, w2_ref),
                (order_hbm, order_ref),
                (gains_hbm, gains_ref),
                (taps_hbm, taps_ref),
            )
        )
    ]
    small[0].start()
    small[1].start()
    chunk = 1024
    copies = [
        pltpu.make_async_copy(
            features_hbm.at[pl.ds(start, chunk)],
            feat.at[pl.ds(side + start, chunk)],
            feat_sem.at[start // chunk],
        )
        for start in range(0, positions, chunk)
    ]
    for copy in copies:
        copy.start()

    barrier = pltpu.get_barrier_semaphore()

    def greet(s, carry):
        pl.semaphore_signal(
            barrier,
            inc=1,
            device_id={"frames": lax.bitwise_xor(me, n - 1 - s)},
            device_id_type=MESH,
        )
        return carry

    lax.fori_loop(0, n - 1, greet, 0, unroll=True)

    for copy in small[2:]:
        copy.start()
    small[0].wait()
    small[1].wait()
    key = jnp.where(frame_ref[...] == me, pos_ref[...], -1).astype(F32)
    key_col = jnp.transpose(jnp.broadcast_to(key, (tracks, tracks)))[:, :1].astype(jnp.int32)
    picked = jnp.zeros((tracks, channels), F32)
    for copy, start in zip(copies, range(0, positions, chunk)):
        chosen = one_hot(iota((tracks, chunk), 1) + start == key_col)
        copy.wait()
        picked = picked + mm(chosen, feat[side + start : side + start + chunk, :])
    copy_p = pltpu.make_async_copy(proj_hbm, proj, local_sem.at[1])
    copy_u = pltpu.make_async_copy(up_hbm, up, local_sem.at[2])
    copy_d = pltpu.make_async_copy(down_hbm, down, local_sem.at[3])
    copy_p.start()
    copy_u.start()
    copy_d.start()

    def scatter_rows(values, slot, owners, count):
        for j in range(per):
            for k in range(count):
                slot[pl.ds(k * per + j, owners, stride=count * per), :] = values[
                    j * owners : (j + 1) * owners, k * LANES : (k + 1) * LANES
                ]
        flat = slot[: owners * count * per, :]
        return flat.reshape(owners, count * per, LANES).astype(BF16)

    def gather_rows(slot, first, owners, count, j, k):
        return slot[pl.ds(first * count * per + k * per + j, owners, stride=count * per), :]

    def gather_all(messages, slot, owners, count):
        slot[: owners * count * per, :] = messages.astype(F32).reshape(
            owners * count * per, LANES
        )
        return jnp.concatenate(
            [
                jnp.concatenate(
                    [gather_rows(slot, 0, owners, count, j, k) for k in range(count)], axis=1
                )
                for j in range(per)
            ],
            axis=0,
        )

    send1[...] = scatter_rows(picked, stage.at[0], n, qc)
    pl.semaphore_wait(barrier, n - 1)
    send_far_first(me, 1, n, lambda t: send1.at[t], recv1, send_sem.at[0], recv_sem.at[0])
    recv1[me] = send1[me]

    for copy in small[2:]:
        copy.wait()
    lane = iota((1, LANES), 1)
    lane_k = lane % ch1
    taps = []
    for tap in range(9):
        vec = jnp.zeros((1, LANES), F32)
        for k in range(ch1):
            vec = jnp.where(lane_k == k, w1_ref[k, tap], vec)
        taps.append(vec)
    bias = jnp.zeros((1, LANES), F32)
    for k in range(ch1):
        bias = jnp.where(lane_k == k, b1_ref[k], bias)
    cells = LANES // ch2
    halves = grid // cells
    groups = halves * pool
    for g in range(groups):
        h, e = g // pool, g % pool
        x_out = (
            (cells * h + lane // (2 * ch1)) * (2 * pool) + 2 * e + (lane // ch1) % 2
        )
        dx = iota((side, LANES), 0) - x_out + 1
        bands = []
        for dy in range(3):
            band = jnp.where(dx == 0, taps[3 * dy], F32(0.0))
            band = jnp.where(dx == 1, taps[3 * dy + 1], band)
            band = jnp.where(dx == 2, taps[3 * dy + 2], band)
            bands.append(band.astype(BF16))
        zero = jnp.zeros((side, LANES), BF16)
        for r in range(4):
            for a in range(2):
                dy = r - a
                toeplitz[g, r * side : (r + 1) * side, a * LANES : (a + 1) * LANES] = (
                    bands[dy] if 0 <= dy < 3 else zero
                )
    wait_messages(n - 1, recv1, recv_sem.at[0])
    mine = jnp.sum(recv1[...].astype(F32), axis=0)
    send2[...] = mine.astype(BF16)
    send_far_first(me, 1, share, lambda t: send2, recv2, send_sem.at[1], recv_sem.at[1])
    send_far_first(me, share, n, lambda t: send2, recv2, send_sem.at[1], recv_sem.at[4])
    recv2[me] = send2[...]

    r = iota((2 * LANES, 4 * ch1), 0)
    s = iota((2 * LANES, 4 * ch1), 1)
    select = one_hot(s == (r % ch1) * 4 + (r // LANES) * 2 + (r // ch1) % 2)
    c_lane = iota((LANES, ch2), 0)
    expand = one_hot(
        iota((LANES, ch2), 1) == (c_lane // (cells * 4)) * 4 + c_lane % 4
    )
    taps2 = mm_nt(mm(select, w2_ref[...]).astype(BF16), expand)
    r = iota((2 * LANES, LANES), 0)
    c = iota((2 * LANES, LANES), 1)
    conv2 = jnp.where((r // (2 * ch1)) % cells == (c // 4) % cells, taps2, 0.0).astype(BF16)

    window_count = grid * grid
    rows = 4 * window_count
    r = iota((rows, rows), 0)
    s = iota((rows, rows), 1)
    reorder = one_hot(s == (r % 4) * window_count + r // 4)
    copy_p.wait()
    for b in range(ch2 // 4):
        moved = mm(reorder, proj[b * rows : (b + 1) * rows, :])
        proj_p[:, b] = moved.astype(BF16).reshape(grid * halves, cells * 4, width)

    rows = n * per
    lane_row = iota((1, rows), 1)
    order = jnp.zeros((1, rows), jnp.int32)
    for f in range(n):
        order = jnp.where(lane_row % n == f, order_ref[f], order)
    place = (order * per + lane_row // n).astype(F32)
    place_col = jnp.transpose(jnp.broadcast_to(place, (rows, rows)))
    earlier_hot = one_hot(place_col - per == place)
    later_hot = one_hot(place_col + per == place)
    links[...] = jnp.concatenate(
        [
            jnp.concatenate([earlier_hot, earlier_hot], axis=1),
            jnp.concatenate([later_hot, later_hot], axis=1),
        ],
        axis=0,
    )

    feat[:side, :] = jnp.zeros((side, channels), BF16)
    feat[side + positions :, :] = jnp.zeros((side, channels), BF16)

    scale = 1.0 / math.sqrt(channels)
    bias2 = jnp.concatenate([bias, bias], axis=1)
    area = pool * pool
    span = 2

    def frame_part(c, owners):
        queries = gather_all(recv2[pl.ds(owners, share)], stage.at[1 + c], share, qc)
        queries = (queries * scale).astype(BF16)
        for start in range(0, positions + LANES, chunk):
            size = min(chunk, positions + LANES - start)
            corr = mm_nt(queries, feat[start : start + size, :]).astype(BF16)
            for j in range(size // LANES):
                blocks[c, start // LANES + j] = corr[:, j * LANES : (j + 1) * LANES]

        pacc[...] = jnp.zeros_like(pacc)
        count = span * pool

        def group(g, carry):
            band = toeplitz[g]
            h = g // pool

            def window(i, carry):
                above = blocks[c, pl.ds(i * count, count)].reshape(count * part, LANES)
                below = blocks[c, pl.ds(i * count + 1, count)].reshape(count * part, LANES)
                first = mm(jnp.concatenate([above, below], axis=1), band) + bias2
                first = jnp.maximum(first.astype(BF16), BF16(0))
                second = jnp.maximum(mm(first, conv2), 0.0)
                second = second.reshape(span, pool, part, LANES)
                for u in range(span):
                    pacc[(i * span + u) * halves + h] += jnp.sum(second[u], axis=0)
                return carry

            return lax.fori_loop(0, grid // span, window, carry, unroll=True)

        lax.fori_loop(0, groups, group, 0, unroll=4)
        pooled = jnp.concatenate(
            [(pacc[j] * (1.0 / area)).astype(BF16) for j in range(grid * halves)], axis=1
        )
        frame_rows = mm(pooled, proj_p[...].reshape(pooled.shape[1], width))
        send3[pl.ds(share - owners, share)] = scatter_rows(
            frame_rows, stage.at[1 + c], share, wc
        )

    wait_messages(share - 1, recv2, recv_sem.at[1])
    frame_part(0, near)
    send_far_first(
        me, share, n, lambda t: send3.at[t], recv3, send_sem.at[2], recv_sem.at[2]
    )
    wait_messages(share, recv2, recv_sem.at[4])
    frame_part(1, far)
    send_far_first(
        me, 1, share, lambda t: send3.at[t], recv3, send_sem.at[2], recv_sem.at[2]
    )
    recv3[me] = send3[me]
    copy_u.wait()
    copy_d.wait()
    wait_messages(n - 1, recv3, recv_sem.at[2])
    state = gather_all(recv3[...], stage.at[3], n, wc)
    for block in range(up.shape[0]):
        normed = norm(state) * gains_ref[block, 0:1, :]
        high = normed.astype(BF16)
        low = (normed - high.astype(F32)).astype(BF16)
        moved = mm(links[...], jnp.concatenate([high, low], axis=0))
        earlier, later = moved[: n * per], moved[n * per :]
        state = (
            state
            + taps_ref[0, pl.ds(block, 1), :] * earlier
            + taps_ref[1, pl.ds(block, 1), :] * normed
            + taps_ref[2, pl.ds(block, 1), :] * later
        )
        inner = (norm(state) * gains_ref[block, 1:2, :]).astype(BF16)
        hidden = jax.nn.gelu(mm(inner, up[block])).astype(BF16)
        state = state + mm(hidden, down[block])
    send4[...] = scatter_rows(state, stage.at[3], n, wc)
    send_far_first(me, 1, n, lambda t: send4.at[t], recv4, send_sem.at[3], recv_sem.at[3])
    recv4[me] = send4[me]
    wait_messages(n - 1, recv4, recv_sem.at[3])
    back = stage.at[4]
    back[...] = recv4[...].astype(F32).reshape(n * wc * per, LANES)
    for j in range(per):
        for half in range(2):
            for k in range(wc):
                rows = gather_rows(back, (1 - half) * share, share, wc, j, k)
                out_ref[
                    pl.ds(j * n + half * share, share), k * LANES : (k + 1) * LANES
                ] = rows.astype(BF16)
    wait_messages(n - 1, recv1, send_sem.at[0])
    wait_messages(n - 1, recv2, send_sem.at[1])
    wait_messages(n - 1, recv3, send_sem.at[2])
    wait_messages(n - 1, recv4, send_sem.at[3])


def on_device(
    features,
    query_frame,
    query_pos,
    frame_order,
    conv1_weight,
    conv1_bias,
    conv2_weight,
    proj_weight,
    norm_gains,
    time_kernels,
    mix_up,
    mix_down,
):
    n = lax.axis_size("frames")
    _, positions, channels = features.shape
    tracks = query_frame.shape[0]
    per = tracks // n
    width = proj_weight.shape[1]
    ch2, ch1 = conv2_weight.shape[:2]
    side = math.isqrt(positions)
    grid = math.isqrt(proj_weight.shape[0] // ch2)
    qc, wc = channels // LANES, width // LANES
    cells = LANES // ch2
    halves = grid // cells
    groups = halves * (side // 2 // grid)
    vmem = pl.BlockSpec(memory_space=pltpu.VMEM)
    hbm = pl.BlockSpec(memory_space=pltpu.HBM)
    out = pl.pallas_call(
        functools.partial(kernel, n, side, grid),
        out_shape=pltpu.VMEM((tracks, width), BF16),
        in_specs=[hbm] * 12,
        out_specs=vmem,
        scratch_shapes=[
            pltpu.VMEM((1, tracks), jnp.int32),
            pltpu.VMEM((1, tracks), jnp.int32),
            pltpu.SMEM(frame_order.shape, jnp.int32),
            pltpu.SMEM(conv1_weight.shape, F32),
            pltpu.SMEM(conv1_bias.shape, F32),
            pltpu.VMEM((ch1 * 4, ch2), BF16),
            pltpu.VMEM(norm_gains.shape, F32),
            pltpu.VMEM((3, norm_gains.shape[0], width), F32),
            pltpu.VMEM((positions + 2 * side, channels), BF16),
            pltpu.VMEM(proj_weight.shape, BF16),
            pltpu.VMEM(mix_up.shape, BF16),
            pltpu.VMEM(mix_down.shape, BF16),
            pltpu.VMEM((grid * halves, ch2 // 4, cells * 4, width), BF16),
            pltpu.VMEM((groups, 4 * side, 2 * LANES), BF16),
            pltpu.VMEM((2, positions // LANES + 1, tracks // 2, LANES), BF16),
            pltpu.VMEM((grid * halves, tracks // 2, LANES), F32),
            pltpu.VMEM((2 * tracks, 2 * tracks), BF16),
            pltpu.VMEM((5, n * wc * per, LANES), F32),
            pltpu.VMEM((n, qc * per, LANES), BF16),
            pltpu.VMEM((n, qc * per, LANES), BF16),
            pltpu.VMEM((qc * per, LANES), BF16),
            pltpu.VMEM((n, qc * per, LANES), BF16),
            pltpu.VMEM((n, wc * per, LANES), BF16),
            pltpu.VMEM((n, wc * per, LANES), BF16),
            pltpu.VMEM((n, wc * per, LANES), BF16),
            pltpu.VMEM((n, wc * per, LANES), BF16),
            pltpu.SemaphoreType.DMA((12,)),
            pltpu.SemaphoreType.DMA((positions // 1024,)),
            pltpu.SemaphoreType.DMA((4,)),
            pltpu.SemaphoreType.DMA((5,)),
        ],
        compiler_params=pltpu.CompilerParams(
            collective_id=0, has_side_effects=True, vmem_limit_bytes=56 * 1024 * 1024
        ),
    )(
        query_frame.reshape(1, tracks),
        query_pos.reshape(1, tracks),
        frame_order,
        conv1_weight,
        conv1_bias,
        conv2_weight.transpose(1, 2, 3, 0).reshape(ch1 * 4, ch2),
        norm_gains,
        time_kernels.transpose(1, 0, 2),
        features.reshape(positions, channels),
        proj_weight,
        mix_up,
        mix_down,
    )
    return out[None]


def solution(mesh):
    placed = (
        P(("groups", "frames"), None, None),
        P("groups"),
        P("groups"),
        P("groups"),
        P(),
        P(),
        P(),
        P(),
        P(),
        P(),
        P(),
        P(),
    )
    return jax.shard_map(
        on_device,
        mesh=mesh,
        in_specs=placed,
        out_specs=P(("groups", "frames"), None, None),
        check_vma=False,
    )
```

```python
import functools
import math

import jax
import jax.numpy as jnp
from jax import lax
from jax.experimental import pallas as pl
from jax.experimental.pallas import tpu as pltpu
from jax.sharding import PartitionSpec as P

F32 = jnp.float32
BF16 = jnp.bfloat16
MESH = pl.DeviceIdType.MESH
LANES = 128


def iota(shape, axis):
    return lax.broadcasted_iota(jnp.int32, shape, axis)


def one_hot(mask):
    return jnp.where(mask, F32(1.0), F32(0.0)).astype(BF16)


def mm(a, b):
    return jnp.dot(a, b, preferred_element_type=F32)


def mm_nt(a, b):
    return lax.dot_general(a, b, (((1,), (1,)), ((), ())), preferred_element_type=F32)


def norm(values):
    center = values - jnp.mean(values, axis=-1, keepdims=True)
    spread = jnp.mean(center * center, axis=-1, keepdims=True)
    return center * lax.rsqrt(spread + 1e-05)


def send_far_first(me, low, high, source, recv, send_sem, recv_sem):
    def step(s, carry):
        target = lax.bitwise_xor(me, high - 1 - s)
        pltpu.make_async_remote_copy(
            src_ref=source(target),
            dst_ref=recv.at[me],
            send_sem=send_sem,
            recv_sem=recv_sem,
            device_id={"frames": target},
            device_id_type=MESH,
        ).start()
        return carry

    lax.fori_loop(0, high - low, step, 0, unroll=True)


def wait_messages(count, ref, sem):
    part = ref.at[pl.ds(0, count)]
    pltpu.make_async_copy(part, part, sem).wait()


def kernel(
    n,
    side,
    grid,
    frame_hbm,
    pos_hbm,
    order_hbm,
    w1_hbm,
    b1_hbm,
    w2_hbm,
    gains_hbm,
    taps_hbm,
    features_hbm,
    proj_hbm,
    up_hbm,
    down_hbm,
    out_ref,
    frame_ref,
    pos_ref,
    order_ref,
    w1_ref,
    b1_ref,
    w2_ref,
    gains_ref,
    taps_ref,
    feat,
    proj,
    up,
    down,
    proj_p,
    toeplitz,
    blocks,
    pacc,
    links,
    stage,
    held,
    held_inner,
    send1,
    recv1,
    send2,
    recv2,
    send3,
    recv3,
    send4,
    recv4,
    local_sem,
    feat_sem,
    send_sem,
    recv_sem,
):
    me = lax.axis_index("frames")
    positions, channels = side * side, feat.shape[1]
    tracks = pos_ref.shape[1]
    per = tracks // n
    ch1 = w1_ref.shape[0]
    ch2 = w2_ref.shape[1]
    width = proj.shape[1]
    hid = up.shape[2]
    qc = channels // LANES
    wc = width // LANES
    half = side // 2
    pool = half // grid
    share = n // 2
    part = tracks // 2
    near = (me // share) * share
    far = share - near

    small = [
        pltpu.make_async_copy(source, target, local_sem.at[4 + i])
        for i, (source, target) in enumerate(
            (
                (frame_hbm, frame_ref),
                (pos_hbm, pos_ref),
                (w1_hbm, w1_ref),
                (b1_hbm, b1_ref),
                (w2_hbm, w2_ref),
                (order_hbm, order_ref),
                (gains_hbm, gains_ref),
                (taps_hbm, taps_ref),
            )
        )
    ]
    small[0].start()
    small[1].start()
    chunk = 1024
    copies = [
        pltpu.make_async_copy(
            features_hbm.at[pl.ds(start, chunk)],
            feat.at[pl.ds(side + start, chunk)],
            feat_sem.at[start // chunk],
        )
        for start in range(0, positions, chunk)
    ]
    for copy in copies:
        copy.start()

    barrier = pltpu.get_barrier_semaphore()

    def greet(s, carry):
        pl.semaphore_signal(
            barrier,
            inc=1,
            device_id={"frames": lax.bitwise_xor(me, n - 1 - s)},
            device_id_type=MESH,
        )
        return carry

    lax.fori_loop(0, n - 1, greet, 0, unroll=True)

    for copy in small[2:]:
        copy.start()
    small[0].wait()
    small[1].wait()
    key = jnp.where(frame_ref[...] == me, pos_ref[...], -1).astype(F32)
    key_col = jnp.transpose(jnp.broadcast_to(key, (tracks, tracks)))[:, :1].astype(jnp.int32)
    picked = jnp.zeros((tracks, channels), F32)
    for copy, start in zip(copies, range(0, positions, chunk)):
        chosen = one_hot(iota((tracks, chunk), 1) + start == key_col)
        copy.wait()
        picked = picked + mm(chosen, feat[side + start : side + start + chunk, :])
    copy_p = pltpu.make_async_copy(proj_hbm, proj, local_sem.at[1])
    copy_u = pltpu.make_async_copy(up_hbm, up, local_sem.at[2])
    copy_d = pltpu.make_async_copy(down_hbm, down, local_sem.at[3])
    copy_p.start()
    copy_u.start()
    copy_d.start()

    def scatter_rows(values, slot, owners, count):
        for j in range(per):
            for k in range(count):
                slot[pl.ds(k * per + j, owners, stride=count * per), :] = values[
                    j * owners : (j + 1) * owners, k * LANES : (k + 1) * LANES
                ]
        flat = slot[: owners * count * per, :]
        return flat.reshape(owners, count * per, LANES).astype(BF16)

    def gather_rows(slot, first, owners, count, j, k):
        return slot[pl.ds(first * count * per + k * per + j, owners, stride=count * per), :]

    def gather_all(messages, slot, owners, count):
        slot[: owners * count * per, :] = messages.astype(F32).reshape(
            owners * count * per, LANES
        )
        return jnp.concatenate(
            [
                jnp.concatenate(
                    [gather_rows(slot, 0, owners, count, j, k) for k in range(count)], axis=1
                )
                for j in range(per)
            ],
            axis=0,
        )

    send1[...] = scatter_rows(picked, stage.at[0], n, qc)
    pl.semaphore_wait(barrier, n - 1)
    send_far_first(me, 1, n, lambda t: send1.at[t], recv1, send_sem.at[0], recv_sem.at[0])
    recv1[me] = send1[me]

    for copy in small[2:]:
        copy.wait()
    lane = iota((1, LANES), 1)
    lane_k = lane % ch1
    taps = []
    for tap in range(9):
        vec = jnp.zeros((1, LANES), F32)
        for k in range(ch1):
            vec = jnp.where(lane_k == k, w1_ref[k, tap], vec)
        taps.append(vec)
    bias = jnp.zeros((1, LANES), F32)
    for k in range(ch1):
        bias = jnp.where(lane_k == k, b1_ref[k], bias)
    cells = LANES // ch2
    halves = grid // cells
    groups = halves * pool
    for g in range(groups):
        h, e = g // pool, g % pool
        x_out = (
            (cells * h + lane // (2 * ch1)) * (2 * pool) + 2 * e + (lane // ch1) % 2
        )
        dx = iota((side, LANES), 0) - x_out + 1
        bands = []
        for dy in range(3):
            band = jnp.where(dx == 0, taps[3 * dy], F32(0.0))
            band = jnp.where(dx == 1, taps[3 * dy + 1], band)
            band = jnp.where(dx == 2, taps[3 * dy + 2], band)
            bands.append(band.astype(BF16))
        zero = jnp.zeros((side, LANES), BF16)
        for r in range(4):
            for a in range(2):
                dy = r - a
                toeplitz[g, r * side : (r + 1) * side, a * LANES : (a + 1) * LANES] = (
                    bands[dy] if 0 <= dy < 3 else zero
                )
    wait_messages(n - 1, recv1, recv_sem.at[0])
    mine = jnp.sum(recv1[...].astype(F32), axis=0)
    send2[...] = mine.astype(BF16)
    send_far_first(me, 1, share, lambda t: send2, recv2, send_sem.at[1], recv_sem.at[1])
    send_far_first(me, share, n, lambda t: send2, recv2, send_sem.at[1], recv_sem.at[4])
    recv2[me] = send2[...]

    r = iota((2 * LANES, 4 * ch1), 0)
    s = iota((2 * LANES, 4 * ch1), 1)
    select = one_hot(s == (r % ch1) * 4 + (r // LANES) * 2 + (r // ch1) % 2)
    c_lane = iota((LANES, ch2), 0)
    expand = one_hot(
        iota((LANES, ch2), 1) == (c_lane // (cells * 4)) * 4 + c_lane % 4
    )
    taps2 = mm_nt(mm(select, w2_ref[...]).astype(BF16), expand)
    r = iota((2 * LANES, LANES), 0)
    c = iota((2 * LANES, LANES), 1)
    conv2 = jnp.where((r // (2 * ch1)) % cells == (c // 4) % cells, taps2, 0.0).astype(BF16)

    window_count = grid * grid
    rows = 4 * window_count
    r = iota((rows, rows), 0)
    s = iota((rows, rows), 1)
    reorder = one_hot(s == (r % 4) * window_count + r // 4)
    copy_p.wait()
    for b in range(ch2 // 4):
        moved = mm(reorder, proj[b * rows : (b + 1) * rows, :])
        proj_p[:, b] = moved.astype(BF16).reshape(grid * halves, cells * 4, width)

    rows = n * per
    lane_row = iota((1, rows), 1)
    order = jnp.zeros((1, rows), jnp.int32)
    for f in range(n):
        order = jnp.where((lane_row // part) * share + lane_row % share == f, order_ref[f], order)
    place = (order * per + (lane_row // share) % per).astype(F32)
    place_col = jnp.transpose(jnp.broadcast_to(place, (rows, rows)))
    earlier_hot = one_hot(place_col - per == place)
    later_hot = one_hot(place_col + per == place)
    links[...] = jnp.concatenate(
        [
            jnp.concatenate([earlier_hot, earlier_hot], axis=1),
            jnp.concatenate([later_hot, later_hot], axis=1),
        ],
        axis=0,
    )

    feat[:side, :] = jnp.zeros((side, channels), BF16)
    feat[side + positions :, :] = jnp.zeros((side, channels), BF16)

    scale = 1.0 / math.sqrt(channels)
    bias2 = jnp.concatenate([bias, bias], axis=1)
    area = pool * pool
    span = 2

    def frame_part(c, owners):
        queries = gather_all(recv2[pl.ds(owners, share)], stage.at[1 + c], share, qc)
        queries = (queries * scale).astype(BF16)
        for start in range(0, positions + LANES, chunk):
            size = min(chunk, positions + LANES - start)
            corr = mm_nt(queries, feat[start : start + size, :]).astype(BF16)
            for j in range(size // LANES):
                blocks[c, start // LANES + j] = corr[:, j * LANES : (j + 1) * LANES]

        pacc[...] = jnp.zeros_like(pacc)
        count = span * pool

        def group(g, carry):
            band = toeplitz[g]
            h = g // pool

            def window(i, carry):
                above = blocks[c, pl.ds(i * count, count)].reshape(count * part, LANES)
                below = blocks[c, pl.ds(i * count + 1, count)].reshape(count * part, LANES)
                first = mm(jnp.concatenate([above, below], axis=1), band) + bias2
                first = jnp.maximum(first.astype(BF16), BF16(0))
                second = jnp.maximum(mm(first, conv2), 0.0)
                second = second.reshape(span, pool, part, LANES)
                for u in range(span):
                    pacc[(i * span + u) * halves + h] += jnp.sum(second[u], axis=0)
                return carry

            return lax.fori_loop(0, grid // span, window, carry, unroll=True)

        lax.fori_loop(0, groups, group, 0, unroll=4)
        pooled = jnp.concatenate(
            [(pacc[j] * (1.0 / area)).astype(BF16) for j in range(grid * halves)], axis=1
        )
        frame_rows = mm(pooled, proj_p[...].reshape(pooled.shape[1], width))
        send3[pl.ds(share - owners, share)] = scatter_rows(
            frame_rows, stage.at[1 + c], share, wc
        )

    wait_messages(share - 1, recv2, recv_sem.at[1])
    frame_part(0, near)
    send_far_first(
        me, share, n, lambda t: send3.at[t], recv3, send_sem.at[2], recv_sem.at[2]
    )
    wait_messages(share, recv2, recv_sem.at[4])
    frame_part(1, far)
    send_far_first(
        me, 1, share, lambda t: send3.at[t], recv3, send_sem.at[2], recv_sem.at[2]
    )
    recv3[me] = send3[me]
    copy_u.wait()
    copy_d.wait()
    wait_messages(n - 1, recv3, recv_sem.at[2])
    state = jnp.concatenate(
        [
            gather_all(recv3[pl.ds(half * share, share)], stage.at[half], share, wc)
            for half in range(2)
        ],
        axis=0,
    )
    for block in range(up.shape[0]):
        normed = norm(state) * gains_ref[block, 0:1, :]
        high = normed.astype(BF16)
        low = (normed - high.astype(F32)).astype(BF16)
        moved = mm(links[...], jnp.concatenate([high, low], axis=0))
        earlier, later = moved[: n * per], moved[n * per :]
        state = (
            state
            + taps_ref[0, pl.ds(block, 1), :] * earlier
            + taps_ref[1, pl.ds(block, 1), :] * normed
            + taps_ref[2, pl.ds(block, 1), :] * later
        )
        inner = (norm(state) * gains_ref[block, 1:2, :]).astype(BF16)
        if block < up.shape[0] - 1:
            hidden = jax.nn.gelu(mm(inner, up[block])).astype(BF16)
            state = state + mm(hidden, down[block])

    held[...] = state.reshape(2, part, width)
    held_inner[...] = inner.reshape(2, part, width)

    def finish(half, low, high, slot):
        hidden = jax.nn.gelu(mm(held_inner[half], up[block])).astype(BF16)
        done = held[half] + mm(hidden, down[block])
        send4[pl.ds(half * share, share)] = scatter_rows(done, slot, share, wc)
        send_far_first(
            me, low, high, lambda t: send4.at[t], recv4, send_sem.at[3], recv_sem.at[3]
        )

    finish(far // share, share, n, stage.at[2])
    finish(near // share, 1, share, stage.at[3])
    recv4[me] = send4[me]
    wait_messages(n - 1, recv4, recv_sem.at[3])
    back = stage.at[4]
    back[...] = recv4[...].astype(F32).reshape(n * wc * per, LANES)
    for j in range(per):
        for half in range(2):
            for k in range(wc):
                rows = gather_rows(back, (1 - half) * share, share, wc, j, k)
                out_ref[
                    pl.ds(j * n + half * share, share), k * LANES : (k + 1) * LANES
                ] = rows.astype(BF16)
    wait_messages(n - 1, recv1, send_sem.at[0])
    wait_messages(n - 1, recv2, send_sem.at[1])
    wait_messages(n - 1, recv3, send_sem.at[2])
    wait_messages(n - 1, recv4, send_sem.at[3])


def on_device(
    features,
    query_frame,
    query_pos,
    frame_order,
    conv1_weight,
    conv1_bias,
    conv2_weight,
    proj_weight,
    norm_gains,
    time_kernels,
    mix_up,
    mix_down,
):
    n = lax.axis_size("frames")
    _, positions, channels = features.shape
    tracks = query_frame.shape[0]
    per = tracks // n
    width = proj_weight.shape[1]
    ch2, ch1 = conv2_weight.shape[:2]
    side = math.isqrt(positions)
    grid = math.isqrt(proj_weight.shape[0] // ch2)
    qc, wc = channels // LANES, width // LANES
    cells = LANES // ch2
    halves = grid // cells
    groups = halves * (side // 2 // grid)
    vmem = pl.BlockSpec(memory_space=pltpu.VMEM)
    hbm = pl.BlockSpec(memory_space=pltpu.HBM)
    out = pl.pallas_call(
        functools.partial(kernel, n, side, grid),
        out_shape=pltpu.VMEM((tracks, width), BF16),
        in_specs=[hbm] * 12,
        out_specs=vmem,
        scratch_shapes=[
            pltpu.VMEM((1, tracks), jnp.int32),
            pltpu.VMEM((1, tracks), jnp.int32),
            pltpu.SMEM(frame_order.shape, jnp.int32),
            pltpu.SMEM(conv1_weight.shape, F32),
            pltpu.SMEM(conv1_bias.shape, F32),
            pltpu.VMEM((ch1 * 4, ch2), BF16),
            pltpu.VMEM(norm_gains.shape, F32),
            pltpu.VMEM((3, norm_gains.shape[0], width), F32),
            pltpu.VMEM((positions + 2 * side, channels), BF16),
            pltpu.VMEM(proj_weight.shape, BF16),
            pltpu.VMEM(mix_up.shape, BF16),
            pltpu.VMEM(mix_down.shape, BF16),
            pltpu.VMEM((grid * halves, ch2 // 4, cells * 4, width), BF16),
            pltpu.VMEM((groups, 4 * side, 2 * LANES), BF16),
            pltpu.VMEM((2, positions // LANES + 1, tracks // 2, LANES), BF16),
            pltpu.VMEM((grid * halves, tracks // 2, LANES), F32),
            pltpu.VMEM((2 * tracks, 2 * tracks), BF16),
            pltpu.VMEM((5, n * wc * per, LANES), F32),
            pltpu.VMEM((2, tracks // 2, width), F32),
            pltpu.VMEM((2, tracks // 2, width), BF16),
            pltpu.VMEM((n, qc * per, LANES), BF16),
            pltpu.VMEM((n, qc * per, LANES), BF16),
            pltpu.VMEM((qc * per, LANES), BF16),
            pltpu.VMEM((n, qc * per, LANES), BF16),
            pltpu.VMEM((n, wc * per, LANES), BF16),
            pltpu.VMEM((n, wc * per, LANES), BF16),
            pltpu.VMEM((n, wc * per, LANES), BF16),
            pltpu.VMEM((n, wc * per, LANES), BF16),
            pltpu.SemaphoreType.DMA((12,)),
            pltpu.SemaphoreType.DMA((positions // 1024,)),
            pltpu.SemaphoreType.DMA((4,)),
            pltpu.SemaphoreType.DMA((5,)),
        ],
        compiler_params=pltpu.CompilerParams(
            collective_id=0, has_side_effects=True, vmem_limit_bytes=56 * 1024 * 1024
        ),
    )(
        query_frame.reshape(1, tracks),
        query_pos.reshape(1, tracks),
        frame_order,
        conv1_weight,
        conv1_bias,
        conv2_weight.transpose(1, 2, 3, 0).reshape(ch1 * 4, ch2),
        norm_gains,
        time_kernels.transpose(1, 0, 2),
        features.reshape(positions, channels),
        proj_weight,
        mix_up,
        mix_down,
    )
    return out[None]


def solution(mesh):
    placed = (
        P(("groups", "frames"), None, None),
        P("groups"),
        P("groups"),
        P("groups"),
        P(),
        P(),
        P(),
        P(),
        P(),
        P(),
        P(),
        P(),
    )
    return jax.shard_map(
        on_device,
        mesh=mesh,
        in_specs=placed,
        out_specs=P(("groups", "frames"), None, None),
        check_vma=False,
    )
```

```python
import functools
import math

import jax
import jax.numpy as jnp
from jax import lax
from jax.experimental import pallas as pl
from jax.experimental.pallas import tpu as pltpu
from jax.sharding import PartitionSpec as P

F32 = jnp.float32
BF16 = jnp.bfloat16
MESH = pl.DeviceIdType.MESH
LANES = 128


def iota(shape, axis):
    return lax.broadcasted_iota(jnp.int32, shape, axis)


def one_hot(mask):
    return jnp.where(mask, F32(1.0), F32(0.0)).astype(BF16)


def mm(a, b):
    return jnp.dot(a, b, preferred_element_type=F32)


def mm_nt(a, b):
    return lax.dot_general(a, b, (((1,), (1,)), ((), ())), preferred_element_type=F32)


def norm(values):
    center = values - jnp.mean(values, axis=-1, keepdims=True)
    spread = jnp.mean(center * center, axis=-1, keepdims=True)
    return center * lax.rsqrt(spread + 1e-05)


def send_far_first(me, low, high, source, recv, send_sem, recv_sem):
    def step(s, carry):
        target = lax.bitwise_xor(me, high - 1 - s)
        pltpu.make_async_remote_copy(
            src_ref=source(target),
            dst_ref=recv.at[me],
            send_sem=send_sem,
            recv_sem=recv_sem,
            device_id={"frames": target},
            device_id_type=MESH,
        ).start()
        return carry

    lax.fori_loop(0, high - low, step, 0, unroll=True)


def wait_messages(count, ref, sem):
    part = ref.at[pl.ds(0, count)]
    pltpu.make_async_copy(part, part, sem).wait()


def kernel(
    n,
    side,
    grid,
    frame_hbm,
    pos_hbm,
    order_hbm,
    w1_hbm,
    b1_hbm,
    w2_hbm,
    gains_hbm,
    taps_hbm,
    features_hbm,
    proj_hbm,
    up_hbm,
    down_hbm,
    out_ref,
    frame_ref,
    pos_ref,
    order_ref,
    w1_ref,
    b1_ref,
    w2_ref,
    gains_ref,
    taps_ref,
    feat,
    proj,
    up,
    down,
    proj_p,
    toeplitz,
    blocks,
    pacc,
    links,
    stage,
    held,
    held_inner,
    send1,
    recv1,
    send2,
    recv2,
    send3,
    recv3,
    send4,
    recv4,
    local_sem,
    feat_sem,
    send_sem,
    recv_sem,
):
    me = lax.axis_index("frames")
    positions, channels = side * side, feat.shape[1]
    tracks = pos_ref.shape[1]
    per = tracks // n
    ch1 = w1_ref.shape[0]
    ch2 = w2_ref.shape[1]
    width = proj.shape[1]
    hid = up.shape[2]
    qc = channels // LANES
    wc = width // LANES
    half = side // 2
    pool = half // grid
    share = n // 2
    part = tracks // 2
    near = (me // share) * share
    far = share - near

    small = [
        pltpu.make_async_copy(source, target, local_sem.at[4 + i])
        for i, (source, target) in enumerate(
            (
                (frame_hbm, frame_ref),
                (pos_hbm, pos_ref),
                (w1_hbm, w1_ref),
                (b1_hbm, b1_ref),
                (w2_hbm, w2_ref),
                (order_hbm, order_ref),
                (gains_hbm, gains_ref),
                (taps_hbm, taps_ref),
            )
        )
    ]
    small[0].start()
    small[1].start()
    chunk = 1024
    copies = [
        pltpu.make_async_copy(
            features_hbm.at[pl.ds(start, chunk)],
            feat.at[pl.ds(side + start, chunk)],
            feat_sem.at[start // chunk],
        )
        for start in range(0, positions, chunk)
    ]
    for copy in copies:
        copy.start()

    barrier = pltpu.get_barrier_semaphore()

    def greet(s, carry):
        pl.semaphore_signal(
            barrier,
            inc=1,
            device_id={"frames": lax.bitwise_xor(me, n - 1 - s)},
            device_id_type=MESH,
        )
        return carry

    lax.fori_loop(0, n - 1, greet, 0, unroll=True)

    for copy in small[2:]:
        copy.start()
    small[0].wait()
    small[1].wait()
    key = jnp.where(frame_ref[...] == me, pos_ref[...], -1).astype(F32)
    key_col = jnp.transpose(jnp.broadcast_to(key, (tracks, tracks)))[:, :1].astype(jnp.int32)
    picked = jnp.zeros((tracks, channels), F32)
    for copy, start in zip(copies, range(0, positions, chunk)):
        chosen = one_hot(iota((tracks, chunk), 1) + start == key_col)
        copy.wait()
        picked = picked + mm(chosen, feat[side + start : side + start + chunk, :])
    copy_p = pltpu.make_async_copy(proj_hbm, proj, local_sem.at[1])
    copy_u = pltpu.make_async_copy(up_hbm, up, local_sem.at[2])
    copy_d = pltpu.make_async_copy(down_hbm, down, local_sem.at[3])
    copy_p.start()
    copy_u.start()
    copy_d.start()

    def scatter_rows(values, slot, owners, count):
        for j in range(per):
            for k in range(count):
                slot[pl.ds(k * per + j, owners, stride=count * per), :] = values[
                    j * owners : (j + 1) * owners, k * LANES : (k + 1) * LANES
                ]
        flat = slot[: owners * count * per, :]
        return flat.reshape(owners, count * per, LANES).astype(BF16)

    def gather_rows(slot, first, owners, count, j, k):
        return slot[pl.ds(first * count * per + k * per + j, owners, stride=count * per), :]

    def gather_all(messages, slot, owners, count):
        slot[: owners * count * per, :] = messages.astype(F32).reshape(
            owners * count * per, LANES
        )
        return jnp.concatenate(
            [
                jnp.concatenate(
                    [gather_rows(slot, 0, owners, count, j, k) for k in range(count)], axis=1
                )
                for j in range(per)
            ],
            axis=0,
        )

    send1[...] = scatter_rows(picked, stage.at[0], n, qc)
    pl.semaphore_wait(barrier, n - 1)
    send_far_first(me, 1, n, lambda t: send1.at[t], recv1, send_sem.at[0], recv_sem.at[0])
    recv1[me] = send1[me]

    for copy in small[2:]:
        copy.wait()
    lane = iota((1, LANES), 1)
    lane_k = lane % ch1
    taps = []
    for tap in range(9):
        vec = jnp.zeros((1, LANES), F32)
        for k in range(ch1):
            vec = jnp.where(lane_k == k, w1_ref[k, tap], vec)
        taps.append(vec)
    bias = jnp.zeros((1, LANES), F32)
    for k in range(ch1):
        bias = jnp.where(lane_k == k, b1_ref[k], bias)
    cells = LANES // ch2
    halves = grid // cells
    groups = halves * pool
    for g in range(groups):
        h, e = g // pool, g % pool
        x_out = (
            (cells * h + lane // (2 * ch1)) * (2 * pool) + 2 * e + (lane // ch1) % 2
        )
        dx = iota((side, LANES), 0) - x_out + 1
        bands = []
        for dy in range(3):
            band = jnp.where(dx == 0, taps[3 * dy], F32(0.0))
            band = jnp.where(dx == 1, taps[3 * dy + 1], band)
            band = jnp.where(dx == 2, taps[3 * dy + 2], band)
            bands.append(band.astype(BF16))
        zero = jnp.zeros((side, LANES), BF16)
        for r in range(4):
            for a in range(2):
                dy = r - a
                toeplitz[g, r * side : (r + 1) * side, a * LANES : (a + 1) * LANES] = (
                    bands[dy] if 0 <= dy < 3 else zero
                )
    wait_messages(n - 1, recv1, recv_sem.at[0])
    mine = jnp.sum(recv1[...].astype(F32), axis=0)
    send2[...] = mine.astype(BF16)
    send_far_first(me, 1, share, lambda t: send2, recv2, send_sem.at[1], recv_sem.at[1])
    send_far_first(me, share, n, lambda t: send2, recv2, send_sem.at[1], recv_sem.at[4])
    recv2[me] = send2[...]

    r = iota((2 * LANES, 4 * ch1), 0)
    s = iota((2 * LANES, 4 * ch1), 1)
    select = one_hot(s == (r % ch1) * 4 + (r // LANES) * 2 + (r // ch1) % 2)
    c_lane = iota((LANES, ch2), 0)
    expand = one_hot(
        iota((LANES, ch2), 1) == (c_lane // (cells * 4)) * 4 + c_lane % 4
    )
    taps2 = mm_nt(mm(select, w2_ref[...]).astype(BF16), expand)
    r = iota((2 * LANES, LANES), 0)
    c = iota((2 * LANES, LANES), 1)
    conv2 = jnp.where((r // (2 * ch1)) % cells == (c // 4) % cells, taps2, 0.0).astype(BF16)

    window_count = grid * grid
    rows = 4 * window_count
    r = iota((rows, rows), 0)
    s = iota((rows, rows), 1)
    reorder = one_hot(s == (r % 4) * window_count + r // 4)
    copy_p.wait()
    for b in range(ch2 // 4):
        moved = mm(reorder, proj[b * rows : (b + 1) * rows, :])
        proj_p[:, b] = moved.astype(BF16).reshape(grid * halves, cells * 4, width)

    rows = n * per
    lane_row = iota((1, rows), 1)
    order = jnp.zeros((1, rows), jnp.int32)
    for f in range(n):
        order = jnp.where((lane_row // part) * share + lane_row % share == f, order_ref[f], order)
    place = (order * per + (lane_row // share) % per).astype(F32)
    place_col = jnp.transpose(jnp.broadcast_to(place, (rows, rows)))
    earlier_hot = one_hot(place_col - per == place)
    later_hot = one_hot(place_col + per == place)
    links[...] = jnp.concatenate(
        [
            jnp.concatenate([earlier_hot, earlier_hot], axis=1),
            jnp.concatenate([later_hot, later_hot], axis=1),
        ],
        axis=0,
    )

    feat[:side, :] = jnp.zeros((side, channels), BF16)
    feat[side + positions :, :] = jnp.zeros((side, channels), BF16)

    scale = 1.0 / math.sqrt(channels)
    bias2 = jnp.concatenate([bias, bias], axis=1)
    area = pool * pool
    span = 2

    def frame_part(c, owners):
        queries = gather_all(recv2[pl.ds(owners, share)], stage.at[1 + c], share, qc)
        queries = (queries * scale).astype(BF16)
        for start in range(0, positions + LANES, chunk):
            size = min(chunk, positions + LANES - start)
            corr = mm_nt(queries, feat[start : start + size, :]).astype(BF16)
            for j in range(size // LANES):
                blocks[c, start // LANES + j] = corr[:, j * LANES : (j + 1) * LANES]

        pacc[...] = jnp.zeros_like(pacc)
        count = span * pool

        def group(g, carry):
            band = toeplitz[g]
            h = g // pool

            def window(i, carry):
                above = blocks[c, pl.ds(i * count, count)].reshape(count * part, LANES)
                below = blocks[c, pl.ds(i * count + 1, count)].reshape(count * part, LANES)
                first = mm(jnp.concatenate([above, below], axis=1), band) + bias2
                first = jnp.maximum(first.astype(BF16), BF16(0))
                second = jnp.maximum(mm(first, conv2), 0.0)
                second = second.reshape(span, pool, part, LANES)
                for u in range(span):
                    pacc[(i * span + u) * halves + h] += jnp.sum(second[u], axis=0)
                return carry

            return lax.fori_loop(0, grid // span, window, carry, unroll=True)

        frame_rows = jnp.zeros((part, width), F32)
        for h in range(halves):
            lax.fori_loop(h * pool, (h + 1) * pool, group, 0, unroll=True)
            cells_done = [i * halves + h for i in range(grid)]
            pooled = jnp.concatenate(
                [(pacc[j] * (1.0 / area)).astype(BF16) for j in cells_done], axis=1
            )
            taken = jnp.concatenate(
                [proj_p[j].reshape(LANES, width) for j in cells_done], axis=0
            )
            frame_rows = frame_rows + mm(pooled, taken)
        send3[pl.ds(share - owners, share)] = scatter_rows(
            frame_rows, stage.at[1 + c], share, wc
        )

    wait_messages(share - 1, recv2, recv_sem.at[1])
    frame_part(0, near)
    send_far_first(
        me, share, n, lambda t: send3.at[t], recv3, send_sem.at[2], recv_sem.at[2]
    )
    wait_messages(share, recv2, recv_sem.at[4])
    frame_part(1, far)
    send_far_first(
        me, 1, share, lambda t: send3.at[t], recv3, send_sem.at[2], recv_sem.at[2]
    )
    recv3[me] = send3[me]
    copy_u.wait()
    copy_d.wait()
    wait_messages(n - 1, recv3, recv_sem.at[2])
    state = jnp.concatenate(
        [
            gather_all(recv3[pl.ds(half * share, share)], stage.at[half], share, wc)
            for half in range(2)
        ],
        axis=0,
    )
    for block in range(up.shape[0]):
        normed = norm(state) * gains_ref[block, 0:1, :]
        high = normed.astype(BF16)
        low = (normed - high.astype(F32)).astype(BF16)
        moved = mm(links[...], jnp.concatenate([high, low], axis=0))
        earlier, later = moved[: n * per], moved[n * per :]
        state = (
            state
            + taps_ref[0, pl.ds(block, 1), :] * earlier
            + taps_ref[1, pl.ds(block, 1), :] * normed
            + taps_ref[2, pl.ds(block, 1), :] * later
        )
        inner = (norm(state) * gains_ref[block, 1:2, :]).astype(BF16)
        if block < up.shape[0] - 1:
            hidden = jax.nn.gelu(mm(inner, up[block])).astype(BF16)
            state = state + mm(hidden, down[block])

    held[...] = state.reshape(2, part, width)
    held_inner[...] = inner.reshape(2, part, width)

    def finish(half, low, high, slot):
        hidden = jax.nn.gelu(mm(held_inner[half], up[block])).astype(BF16)
        done = held[half] + mm(hidden, down[block])
        send4[pl.ds(half * share, share)] = scatter_rows(done, slot, share, wc)
        send_far_first(
            me, low, high, lambda t: send4.at[t], recv4, send_sem.at[3], recv_sem.at[3]
        )

    finish(far // share, share, n, stage.at[2])
    finish(near // share, 1, share, stage.at[3])
    recv4[me] = send4[me]
    wait_messages(n - 1, recv4, recv_sem.at[3])
    back = stage.at[4]
    back[...] = recv4[...].astype(F32).reshape(n * wc * per, LANES)
    for j in range(per):
        for half in range(2):
            for k in range(wc):
                rows = gather_rows(back, (1 - half) * share, share, wc, j, k)
                out_ref[
                    pl.ds(j * n + half * share, share), k * LANES : (k + 1) * LANES
                ] = rows.astype(BF16)
    wait_messages(n - 1, recv1, send_sem.at[0])
    wait_messages(n - 1, recv2, send_sem.at[1])
    wait_messages(n - 1, recv3, send_sem.at[2])
    wait_messages(n - 1, recv4, send_sem.at[3])


def on_device(
    features,
    query_frame,
    query_pos,
    frame_order,
    conv1_weight,
    conv1_bias,
    conv2_weight,
    proj_weight,
    norm_gains,
    time_kernels,
    mix_up,
    mix_down,
):
    n = lax.axis_size("frames")
    _, positions, channels = features.shape
    tracks = query_frame.shape[0]
    per = tracks // n
    width = proj_weight.shape[1]
    ch2, ch1 = conv2_weight.shape[:2]
    side = math.isqrt(positions)
    grid = math.isqrt(proj_weight.shape[0] // ch2)
    qc, wc = channels // LANES, width // LANES
    cells = LANES // ch2
    halves = grid // cells
    groups = halves * (side // 2 // grid)
    vmem = pl.BlockSpec(memory_space=pltpu.VMEM)
    hbm = pl.BlockSpec(memory_space=pltpu.HBM)
    out = pl.pallas_call(
        functools.partial(kernel, n, side, grid),
        out_shape=pltpu.VMEM((tracks, width), BF16),
        in_specs=[hbm] * 12,
        out_specs=vmem,
        scratch_shapes=[
            pltpu.VMEM((1, tracks), jnp.int32),
            pltpu.VMEM((1, tracks), jnp.int32),
            pltpu.SMEM(frame_order.shape, jnp.int32),
            pltpu.SMEM(conv1_weight.shape, F32),
            pltpu.SMEM(conv1_bias.shape, F32),
            pltpu.VMEM((ch1 * 4, ch2), BF16),
            pltpu.VMEM(norm_gains.shape, F32),
            pltpu.VMEM((3, norm_gains.shape[0], width), F32),
            pltpu.VMEM((positions + 2 * side, channels), BF16),
            pltpu.VMEM(proj_weight.shape, BF16),
            pltpu.VMEM(mix_up.shape, BF16),
            pltpu.VMEM(mix_down.shape, BF16),
            pltpu.VMEM((grid * halves, ch2 // 4, cells * 4, width), BF16),
            pltpu.VMEM((groups, 4 * side, 2 * LANES), BF16),
            pltpu.VMEM((2, positions // LANES + 1, tracks // 2, LANES), BF16),
            pltpu.VMEM((grid * halves, tracks // 2, LANES), F32),
            pltpu.VMEM((2 * tracks, 2 * tracks), BF16),
            pltpu.VMEM((5, n * wc * per, LANES), F32),
            pltpu.VMEM((2, tracks // 2, width), F32),
            pltpu.VMEM((2, tracks // 2, width), BF16),
            pltpu.VMEM((n, qc * per, LANES), BF16),
            pltpu.VMEM((n, qc * per, LANES), BF16),
            pltpu.VMEM((qc * per, LANES), BF16),
            pltpu.VMEM((n, qc * per, LANES), BF16),
            pltpu.VMEM((n, wc * per, LANES), BF16),
            pltpu.VMEM((n, wc * per, LANES), BF16),
            pltpu.VMEM((n, wc * per, LANES), BF16),
            pltpu.VMEM((n, wc * per, LANES), BF16),
            pltpu.SemaphoreType.DMA((12,)),
            pltpu.SemaphoreType.DMA((positions // 1024,)),
            pltpu.SemaphoreType.DMA((4,)),
            pltpu.SemaphoreType.DMA((5,)),
        ],
        compiler_params=pltpu.CompilerParams(
            collective_id=0, has_side_effects=True, vmem_limit_bytes=56 * 1024 * 1024
        ),
    )(
        query_frame.reshape(1, tracks),
        query_pos.reshape(1, tracks),
        frame_order,
        conv1_weight,
        conv1_bias,
        conv2_weight.transpose(1, 2, 3, 0).reshape(ch1 * 4, ch2),
        norm_gains,
        time_kernels.transpose(1, 0, 2),
        features.reshape(positions, channels),
        proj_weight,
        mix_up,
        mix_down,
    )
    return out[None]


def solution(mesh):
    placed = (
        P(("groups", "frames"), None, None),
        P("groups"),
        P("groups"),
        P("groups"),
        P(),
        P(),
        P(),
        P(),
        P(),
        P(),
        P(),
        P(),
    )
    return jax.shard_map(
        on_device,
        mesh=mesh,
        in_specs=placed,
        out_specs=P(("groups", "frames"), None, None),
        check_vma=False,
    )
```
